32 devices in a mesh: tok: 2 (over x), head: 16 (over z, y, core).
Axes of the slice: x: 2, y: 2, z: 4, core: 2. Of those that a mesh axis runs over, the one named last changes fastest.
Arguments:
- query_states: bfloat16 [4096, 4096], P(('tok', 'head')), may hold values from -7.5 to 7.5
- key_states: bfloat16 [4096, 4096], P(('tok', 'head')), may hold values from -7.5 to 7.5
- value_states: bfloat16 [4096, 4096], P(('tok', 'head')), may hold values from -6 to 6
- token_rates: float32 [16, 4096], P('head', 'tok'), may hold values from 0.05 to 1
- fast_weights: bfloat16 [16, 512, 768], P('head'), may hold values from -0.375 to 0.375
Outputs:
- combined: bfloat16 [4096, 4096], P(('tok', 'head'))
- new_weights: bfloat16 [16, 512, 768], P('head', 'tok')
The draws below stay inside these ranges and needn't reach their ends.
All inputs are finite; a program needn't handle non-finite values.
Results may differ from the reference program's by a relative error of at most 0.039.
Values may be sent and summed in bfloat16 or wider, within the bound.
A program may use at most 64 MiB of HBM per device.

```python
import math
import jax
import jax.numpy as jnp
from jax import lax

DH = 256
FH = 512
WINDOW = 1024
NS_STEPS = 5
TOK_DEV = 2048
HEADS = 16
D = 4096
TOKENS = 4096


def draw_query_states(key, part):
    own_key = jax.random.fold_in(key, 1)
    states = jnp.clip(jax.random.normal(own_key, (TOKENS, D), jnp.float32), -6.0, 6.0)
    return states.astype(jnp.bfloat16)


def draw_key_states(key, part):
    own_key = jax.random.fold_in(key, 2)
    states = jnp.clip(jax.random.normal(own_key, (TOKENS, D), jnp.float32), -6.0, 6.0)
    return states.astype(jnp.bfloat16)


def steps_of(key, shape, shards, smallest, largest):
    level = 1.0
    for dim, shards_of in shards:
        draws = jax.random.uniform(jax.random.fold_in(jax.random.fold_in(key, 6), dim), (shards_of,), jnp.float32, smallest / len(shards), largest / len(shards))
        level = level * jnp.repeat(jnp.exp(draws), shape[dim] // shards_of).reshape((-1,) + (1,) * (len(shape) - 1 - dim))
    return level


def scatter_about(rng, extent, deviation, most, split=(), kind=jnp.bfloat16):
    entries = jax.random.normal(rng, extent, jnp.float32) * deviation
    if len(split) > 0:
        entries = steps_of(rng, extent, split, -0.22, 0.18) * entries
    return jnp.clip(entries, min=-most, max=most).astype(kind)


def setup_inputs(seed: int = 0) -> dict:
    streams_of = jax.random.split(jax.random.key(seed), 6)
    query_states = draw_query_states(jax.random.fold_in(streams_of[5], 71), 0)
    key_states = draw_key_states(jax.random.fold_in(streams_of[5], 71), 0)
    value_states = scatter_about(streams_of[2], (TOKENS, D), 1.0, 6.0, ((0, 32),))
    token_rates = jnp.clip(jnp.exp(math.log(1.0) - 2.9957323 * jax.random.uniform(streams_of[3], (HEADS, TOKENS), jnp.float32) ** steps_of(streams_of[3], (HEADS, TOKENS), ((0, 16), (1, 2)), -0.2, 0.2)), 0.05, 1.0)
    fast_weights = scatter_about(streams_of[4], (HEADS, FH, 3 * DH), DH ** -0.5, 0.375, ((0, 16),))
    return {"query_states": query_states, "key_states": key_states, "value_states": value_states, "token_rates": token_rates, "fast_weights": fast_weights}


coef_linear = 3.4445
coef_cubic = -4.775
coef_quintic = 2.0315
epsilon = 1e-06

def block_size(local_rows):
    return 512 if local_rows % 512 == 0 else local_rows

def rms_norm(values):
    return values * lax.rsqrt(lax.optimization_barrier(jnp.mean(values * values, axis=-1, keepdims=True)) + epsilon)

def silu_parts(gate_value):
    sigmoid = jax.nn.sigmoid(gate_value)
    return (gate_value * sigmoid, sigmoid * (1.0 + gate_value * (1.0 - sigmoid)))

def project(inputs, weights):
    gate_value = jnp.dot(inputs, weights[:, :DH].T, preferred_element_type=jnp.float32)
    up_value = jnp.dot(inputs, weights[:, DH:2 * DH].T, preferred_element_type=jnp.float32)
    return (gate_value, up_value)

def attend(query_rows, key_rows, value_rows, positions, key_positions):
    scores = jnp.dot(query_rows, key_rows.T, preferred_element_type=jnp.float32) * DH ** (-0.5)
    offset = positions[:, None] - key_positions[None, :]
    allowed = (offset >= 0) & (offset < WINDOW) & (key_positions[None, :] >= 0)
    scores = jnp.where(allowed, scores, -1e+30)
    highest = lax.optimization_barrier(jnp.max(scores, axis=1, keepdims=True))
    expo = jnp.exp(scores - highest)
    probs = (expo / lax.optimization_barrier(jnp.sum(expo, axis=1, keepdims=True))).astype(jnp.bfloat16)
    return jnp.dot(probs, value_rows, preferred_element_type=jnp.float32)

def attention_head(query_rows, key_rows, value_rows):
    block_rows = block_size(TOK_DEV)
    padded_keys = jnp.concatenate([jnp.zeros((WINDOW, DH), jnp.bfloat16), key_rows])
    padded_values = jnp.concatenate([jnp.zeros((WINDOW, DH), jnp.bfloat16), value_rows])

    def attend_block(block_index):
        offset = (block_index * block_rows).astype(jnp.int32)
        queries_here = lax.dynamic_slice_in_dim(query_rows, offset, block_rows, 0)
        keys_here = lax.dynamic_slice_in_dim(padded_keys, offset, block_rows + WINDOW, 0)
        values_here = lax.dynamic_slice_in_dim(padded_values, offset, block_rows + WINDOW, 0)
        positions = offset + jnp.arange(block_rows).astype(jnp.int32)
        key_positions = offset - WINDOW + jnp.arange(block_rows + WINDOW).astype(jnp.int32)
        return attend(queries_here, keys_here, values_here, positions, key_positions)
    blocks = lax.map(attend_block, jnp.arange(TOKENS // block_rows).astype(jnp.int32))
    return blocks.reshape(TOKENS, DH)

def newton_schulz(gradient):
    squares = lax.optimization_barrier(jnp.sum(gradient * gradient, axis=(0, 2)))
    iterate = (gradient * lax.rsqrt(squares + epsilon)[None, :, None]).astype(jnp.bfloat16)
    for repeat_index in range(NS_STEPS):
        wide = iterate.astype(jnp.float32)
        gram_matrix = jnp.einsum('fjd,fje->jde', wide, wide, precision=lax.Precision.HIGHEST).astype(jnp.bfloat16)
        gram_wide = gram_matrix.astype(jnp.float32)
        square_gram = jnp.einsum('jde,jef->jdf', gram_wide, gram_wide, precision=lax.Precision.HIGHEST)
        polynomial = (coef_cubic * gram_wide + coef_quintic * square_gram).astype(jnp.bfloat16)
        iterate = (coef_linear * wide + jnp.einsum('fjd,jde->fje', wide, polynomial.astype(jnp.float32), precision=lax.Precision.HIGHEST)).astype(jnp.bfloat16)
    return iterate

def fast_head(query_rows, key_rows, value_rows, rate_rows, weights):
    gate_value, up_value = project(key_rows, weights)
    gate_silu, gate_slope = silu_parts(gate_value)
    hidden = (gate_silu * up_value).astype(jnp.bfloat16)
    target = (-rate_rows[:, None] * value_rows.astype(jnp.float32)).astype(jnp.bfloat16)
    back_grad = jnp.dot(target, weights[:, 2 * DH:].T, preferred_element_type=jnp.float32)
    gate_grad = (back_grad * up_value * gate_slope).astype(jnp.bfloat16)
    up_grad = (back_grad * gate_silu).astype(jnp.bfloat16)
    gradient = jnp.concatenate([jnp.dot(gate_grad.T, key_rows, preferred_element_type=jnp.float32), jnp.dot(up_grad.T, key_rows, preferred_element_type=jnp.float32), jnp.dot(hidden.T, target, preferred_element_type=jnp.float32)], axis=1)
    iterate = newton_schulz(gradient.reshape(FH, 3, DH))
    updated = (weights.reshape(FH, 3, DH).astype(jnp.float32) - iterate.astype(jnp.float32)).astype(jnp.bfloat16).reshape(FH, 3 * DH)
    query_gate, query_up = project(query_rows, updated)
    query_hidden = (jax.nn.silu(query_gate) * query_up).astype(jnp.bfloat16)
    applied = jnp.dot(query_hidden, updated[:, 2 * DH:], preferred_element_type=jnp.float32)
    return (rms_norm(applied), updated)

def reference(query_states, key_states, value_states, token_rates, fast_weights):

    def split_heads(states):
        return states.reshape(TOKENS, HEADS, DH).transpose(1, 0, 2)

    def per_head(items):
        query_rows, key_rows, value_rows, rate_rows, weights = items
        attended = rms_norm(attention_head(query_rows, key_rows, value_rows))
        applied, updated = fast_head(query_rows, key_rows, value_rows, rate_rows, weights)
        return ((attended + applied).astype(jnp.bfloat16), updated)
    combined, new_weights = lax.map(per_head, (split_heads(query_states), split_heads(key_states), split_heads(value_states), token_rates, fast_weights))
    return (combined.transpose(1, 0, 2).reshape(TOKENS, D), new_weights)
```

```python
import functools

import jax
import jax.numpy as jnp
from jax import lax
from jax.experimental import pallas as pl
from jax.experimental.pallas import tpu as pltpu
from jax.sharding import PartitionSpec as P

DH = 256
FH = 512
WINDOW = 1024
NS_STEPS = 5

coef_linear = 3.4445
coef_cubic = -4.775
coef_quintic = 2.0315
epsilon = 1e-06
LOG2E = 1.4426950408889634
MASKED = -1e30
MESH = pl.DeviceIdType.MESH


def dot_nt(left, right):
    return lax.dot_general(
        left, right, (((1,), (1,)), ((), ())), preferred_element_type=jnp.float32
    )


def dot_nn(left, right):
    return lax.dot_general(
        left, right, (((1,), (0,)), ((), ())), preferred_element_type=jnp.float32
    )


def rms_norm(values):
    return values * lax.rsqrt(jnp.mean(values * values, axis=-1, keepdims=True) + epsilon)


def sigmoid(values):
    return 1.0 / (1.0 + jnp.exp(-values))


def turned(values):
    return values.astype(jnp.float32).T.astype(jnp.bfloat16)


def layer_kernel(
    n_tok, n_head, q_hbm, k_hbm, v_hbm, rate_ref, w_ref,
    out_hbm, neww_ref,
    kw, vw, qw, rs, att, acc, grads, zs, wnew, obuf,
    own_sem, k_send, k_recv, v_send, v_recv, q_send, q_recv, o_send, o_recv,
    hk_send, hk_recv, hv_send, hv_recv, g_send, g_recv,
):
    tok = lax.axis_index("tok")
    me = lax.axis_index("head")
    rd = q_hbm.shape[0]
    rg = 2 * rd
    groups = n_head // 2
    halo_groups = WINDOW // rg
    mine = lax.div(me, 2)
    early = max(groups - 2, 1)

    barrier = pltpu.get_barrier_semaphore()

    @pl.loop(1, n_head)
    def _(step):
        pl.semaphore_signal(
            barrier, inc=1, device_id=(tok, lax.rem(me + step, n_head)), device_id_type=MESH
        )

    @pl.loop(1, n_tok)
    def _(step):
        pl.semaphore_signal(
            barrier, inc=1, device_id=(lax.rem(tok + step, n_tok), me), device_id_type=MESH
        )

    def rows_of(index, size, base=0):
        return pl.ds(pl.multiple_of(base + index * size, size), size)

    def cols_of(index):
        return pl.ds(pl.multiple_of(index * DH, DH), DH)

    def scatter(src, dst, base, send, recv, source, target):
        return pltpu.make_async_remote_copy(
            src_ref=src.at[:, cols_of(target)],
            dst_ref=dst.at[rows_of(source, rd, base)],
            send_sem=send.at[target],
            recv_sem=recv.at[source],
            device_id=(tok, target),
            device_id_type=MESH,
        )

    def k_copy(source, target):
        return scatter(k_hbm, kw, WINDOW, k_send, k_recv, source, target)

    def v_copy(source, target):
        return scatter(v_hbm, vw, WINDOW, v_send, v_recv, source, target)

    def q_copy(source, target):
        return scatter(q_hbm, qw, 0, q_send, q_recv, source, target)

    def o_copy(source, target):
        return pltpu.make_async_remote_copy(
            src_ref=obuf.at[rows_of(target, rd)],
            dst_ref=out_hbm.at[:, cols_of(source)],
            send_sem=o_send.at[target],
            recv_sem=o_recv.at[source],
            device_id=(tok, target),
            device_id_type=MESH,
        )

    own_copies = (
        pltpu.make_async_copy(
            k_hbm.at[:, cols_of(me)], kw.at[rows_of(me, rd, WINDOW)], own_sem.at[0]
        ),
        pltpu.make_async_copy(
            v_hbm.at[:, cols_of(me)], vw.at[rows_of(me, rd, WINDOW)], own_sem.at[1]
        ),
        pltpu.make_async_copy(q_hbm.at[:, cols_of(me)], qw.at[rows_of(me, rd)], own_sem.at[2]),
    )
    for copy in own_copies:
        copy.start()

    pl.semaphore_wait(barrier, n_head - 1 + n_tok - 1)

    @pl.loop(1, n_head)
    def _(step):
        target = lax.rem(me + step, n_head)
        k_copy(me, target).start()
        v_copy(me, target).start()

    @pl.loop(1, n_head)
    def _(step):
        q_copy(me, lax.rem(me + step, n_head)).start()

    acc[...] = jnp.zeros_like(acc)

    @pl.when(tok == 0)
    def _():
        kw[0:WINDOW, :] = jnp.zeros((WINDOW, DH), jnp.bfloat16)
        vw[0:WINDOW, :] = jnp.zeros((WINDOW, DH), jnp.bfloat16)

    @pl.loop(0, rs.shape[0] // 128)
    def _(index):
        part = rate_ref[:, rows_of(index, 128)]
        rs[rows_of(index, 128), :] = -jnp.broadcast_to(part, (128, 128)).T

    for copy in own_copies:
        copy.wait()

    def halo_copy(local, halo, send, recv, part):
        return pltpu.make_async_remote_copy(
            src_ref=local.at[rows_of(part + groups, rg)],
            dst_ref=halo.at[rows_of(part, rg)],
            send_sem=send.at[part],
            recv_sem=recv.at[part],
            device_id=(jnp.minimum(tok + 1, n_tok - 1), me),
            device_id_type=MESH,
        )

    def hk_copy(part):
        return halo_copy(kw, kw, hk_send, hk_recv, part)

    def hv_copy(part):
        return halo_copy(vw, vw, hv_send, hv_recv, part)

    def group_at(step):
        return lax.rem(mine - step + groups, groups)

    def wait_group(group, copies):
        for core in range(2):
            source = group * 2 + core

            @pl.when(source != me)
            def _():
                for copy in copies:
                    copy(source, me).wait_recv()

    @pl.loop(0, groups)
    def _(step):
        group = group_at(step)
        wait_group(group, (k_copy, v_copy))
        part = group - (groups - halo_groups)

        @pl.when(jnp.logical_and(part >= 0, tok < n_tok - 1))
        def _():
            hk_copy(part).start()
            hv_copy(part).start()

        keys = kw[rows_of(group, rg, WINDOW), :]
        values = vw[rows_of(group, rg, WINDOW), :].astype(jnp.float32)
        rates = rs[rows_of(group, rg), :]
        target = jnp.concatenate(
            [values[:, :128] * rates, values[:, 128:] * rates], axis=1
        )
        target = target.astype(jnp.bfloat16)
        gate = dot_nt(keys, w_ref[0, :, 0:DH])
        up = dot_nt(keys, w_ref[0, :, DH : 2 * DH])
        back = dot_nt(target, w_ref[0, :, 2 * DH :])
        sig = sigmoid(gate)
        silu = gate * sig
        slope = sig * (1.0 + gate * (1.0 - sig))
        hidden = (silu * up).astype(jnp.bfloat16)
        gate_grad = (back * up * slope).astype(jnp.bfloat16)
        up_grad = (back * silu).astype(jnp.bfloat16)
        keys_t = turned(keys)
        acc[0] += dot_nn(keys_t, gate_grad)
        acc[1] += dot_nn(keys_t, up_grad)
        acc[2] += dot_nn(turned(target), hidden)

    def g_copy(source, target):
        return pltpu.make_async_remote_copy(
            src_ref=grads.at[source],
            dst_ref=grads.at[source],
            send_sem=g_send.at[target],
            recv_sem=g_recv.at[source],
            device_id=(target, me),
            device_id_type=MESH,
        )

    grads[tok] = acc[...].astype(jnp.bfloat16)

    @pl.loop(1, n_tok)
    def _(step):
        g_copy(tok, lax.rem(tok + step, n_tok)).start()

    @pl.when(tok > 0)
    def _():
        @pl.loop(0, halo_groups)
        def _(part):
            hk_copy(part).wait_recv()
            hv_copy(part).wait_recv()

    row = lax.broadcasted_iota(jnp.int32, (rg, rg), 0)
    col = lax.broadcasted_iota(jnp.int32, (rg, rg), 1)

    def attend(group):
        wait_group(group, (q_copy,))
        queries = qw[rows_of(group, rg), :]
        scores = []
        for chunk in range(halo_groups + 1):
            value = dot_nt(queries, kw[rows_of(group + chunk, rg), :])
            if chunk == 0:
                value = jnp.where(col > row, value, MASKED)
            if chunk == halo_groups:
                value = jnp.where(col <= row, value, MASKED)
            else:
                seen = jnp.logical_or(tok > 0, group + chunk >= halo_groups)
                value = value + jnp.where(seen, 0.0, MASKED)
            scores.append(value)
        highest = functools.reduce(jnp.maximum, scores)
        highest = jnp.max(highest, axis=1, keepdims=True)
        total = jnp.zeros((rg, rg), jnp.float32)
        result = jnp.zeros((rg, DH), jnp.float32)
        for chunk in range(halo_groups + 1):
            expo = jnp.exp2((scores[chunk] - highest) * (LOG2E * DH ** (-0.5)))
            total = total + expo
            result = result + dot_nn(
                expo.astype(jnp.bfloat16), vw[rows_of(group + chunk, rg), :]
            )
        result = result / jnp.sum(total, axis=1, keepdims=True)
        att[rows_of(group, rg), :] = rms_norm(result)

    @pl.loop(0, early)
    def _(step):
        attend(group_at(step))

    @pl.loop(1, n_tok)
    def _(step):
        g_copy(lax.rem(tok + step, n_tok), tok).wait_recv()

    for block in range(3):
        total = grads[0, block].astype(jnp.float32)
        for index in range(1, n_tok):
            total = total + grads[index, block].astype(jnp.float32)
        squares = jnp.sum(
            jnp.sum(total * total, axis=1, keepdims=True), axis=0, keepdims=True
        )
        zs[block] = (total * lax.rsqrt(squares + epsilon)).astype(jnp.bfloat16)

    @pl.loop(0, NS_STEPS)
    def _(step):
        blocks = [zs[block] for block in range(3)]
        grams = [dot_nt(z, z).astype(jnp.bfloat16) for z in blocks]
        polys = [
            (coef_cubic * a.astype(jnp.float32) + coef_quintic * dot_nn(a, a)).astype(
                jnp.bfloat16
            )
            for a in grams
        ]
        for block in range(3):
            zs[block] = (
                coef_linear * blocks[block].astype(jnp.float32)
                + dot_nn(polys[block], blocks[block])
            ).astype(jnp.bfloat16)

    for block in range(3):
        columns = slice(block * DH, (block + 1) * DH)
        wnew[:, columns] = (
            w_ref[0, :, columns].astype(jnp.float32) - zs[block].astype(jnp.float32).T
        ).astype(jnp.bfloat16)

    @pl.loop(1, groups + 1)
    def _(step):
        group = group_at(step)

        @pl.when(jnp.logical_and(step >= early, step < groups))
        def _():
            attend(group)

        queries = qw[rows_of(group, rg), :]
        gate = dot_nt(queries, wnew[:, 0:DH])
        up = dot_nt(queries, wnew[:, DH : 2 * DH])
        hidden = (gate * sigmoid(gate) * up).astype(jnp.bfloat16)
        applied = rms_norm(dot_nn(hidden, wnew[:, 2 * DH :]))
        obuf[rows_of(group, rg), :] = (att[rows_of(group, rg), :] + applied).astype(
            jnp.bfloat16
        )
        for core in range(2):
            target = group * 2 + core

            @pl.when(target != me)
            def _():
                o_copy(me, target).start()

    own_out = pltpu.make_async_copy(
        obuf.at[rows_of(me, rd)], out_hbm.at[:, cols_of(me)], own_sem.at[3]
    )
    own_out.start()
    owned = FH // n_tok
    neww_ref[0] = wnew[rows_of(tok, owned), :]

    @pl.loop(1, n_head)
    def _(step):
        target = lax.rem(me + step, n_head)
        k_copy(me, target).wait_send()
        v_copy(me, target).wait_send()
        q_copy(me, target).wait_send()
        o_copy(me, target).wait_send()

    @pl.loop(1, n_tok)
    def _(step):
        g_copy(tok, lax.rem(tok + step, n_tok)).wait_send()

    @pl.when(tok < n_tok - 1)
    def _():
        @pl.loop(0, halo_groups)
        def _(part):
            hk_copy(part).wait_send()
            hv_copy(part).wait_send()

    @pl.loop(1, n_head)
    def _(step):
        o_copy(lax.rem(me + step, n_head), me).wait_recv()

    own_out.wait()


def per_device(query_states, key_states, value_states, token_rates, fast_weights):
    n_tok = lax.axis_size("tok")
    n_head = lax.axis_size("head")
    rd, width = query_states.shape
    rows = rd * n_head
    halo_groups = WINDOW // (2 * rd)
    dma = pltpu.SemaphoreType.DMA
    heads_sems = [dma((n_head,))] * 8
    return pl.pallas_call(
        functools.partial(layer_kernel, n_tok, n_head),
        out_shape=(
            jax.ShapeDtypeStruct((rd, width), jnp.bfloat16),
            jax.ShapeDtypeStruct((1, FH // n_tok, 3 * DH), jnp.bfloat16),
        ),
        in_specs=[pl.BlockSpec(memory_space=pl.ANY)] * 3
        + [pl.BlockSpec(memory_space=pltpu.VMEM)] * 2,
        out_specs=(
            pl.BlockSpec(memory_space=pl.ANY),
            pl.BlockSpec(memory_space=pltpu.VMEM),
        ),
        scratch_shapes=[
            pltpu.VMEM((WINDOW + rows, DH), jnp.bfloat16),
            pltpu.VMEM((WINDOW + rows, DH), jnp.bfloat16),
            pltpu.VMEM((rows, DH), jnp.bfloat16),
            pltpu.VMEM((rows, 128), jnp.float32),
            pltpu.VMEM((rows, DH), jnp.float32),
            pltpu.VMEM((3, DH, FH), jnp.float32),
            pltpu.VMEM((n_tok, 3, DH, FH), jnp.bfloat16),
            pltpu.VMEM((3, DH, FH), jnp.bfloat16),
            pltpu.VMEM((FH, 3 * DH), jnp.bfloat16),
            pltpu.VMEM((rows, DH), jnp.bfloat16),
            dma((4,)),
            *heads_sems,
            dma((halo_groups,)),
            dma((halo_groups,)),
            dma((halo_groups,)),
            dma((halo_groups,)),
            dma((n_tok,)),
            dma((n_tok,)),
        ],
        compiler_params=pltpu.CompilerParams(
            collective_id=0, has_side_effects=True, vmem_limit_bytes=60 * 1024 * 1024
        ),
        name="layer",
    )(query_states, key_states, value_states, token_rates, fast_weights)


def solution(mesh):
    return jax.shard_map(
        per_device,
        mesh=mesh,
        in_specs=(
            P(("tok", "head"), None),
            P(("tok", "head"), None),
            P(("tok", "head"), None),
            P("head", "tok"),
            P("head", None, None),
        ),
        out_specs=(P(("tok", "head"), None), P("head", "tok", None)),
        check_vma=False,
    )
```

```python
import functools

import jax
import jax.numpy as jnp
from jax import lax
from jax.experimental import pallas as pl
from jax.experimental.pallas import tpu as pltpu
from jax.sharding import PartitionSpec as P

DH = 256
FH = 512
WINDOW = 1024
NS_STEPS = 5

coef_linear = 3.4445
coef_cubic = -4.775
coef_quintic = 2.0315
epsilon = 1e-06
LOG2E = 1.4426950408889634
MASKED = -1e30
MESH = pl.DeviceIdType.MESH


def dot_nt(left, right):
    return lax.dot_general(
        left, right, (((1,), (1,)), ((), ())), preferred_element_type=jnp.float32
    )


def dot_nn(left, right):
    return lax.dot_general(
        left, right, (((1,), (0,)), ((), ())), preferred_element_type=jnp.float32
    )


def rms_norm(values):
    return values * lax.rsqrt(jnp.mean(values * values, axis=-1, keepdims=True) + epsilon)


def sigmoid(values):
    return 1.0 / (1.0 + jnp.exp(-values))


def turned(values):
    return values.astype(jnp.float32).T.astype(jnp.bfloat16)


def layer_kernel(
    n_tok, n_head, q_hbm, k_hbm, v_hbm, rate_ref, w_ref,
    out_hbm, neww_ref,
    kv, qw, rates, acc, zs, wnew, obuf,
    own_sem, k_send, k_recv, v_send, v_recv, q_send, q_recv, o_send, o_recv,
    f_send, f_recv, r_send, r_recv,
):
    tok = lax.axis_index("tok")
    me = lax.axis_index("head")
    rd = q_hbm.shape[0]
    rg = 2 * rd
    groups = n_head // 2
    halo_groups = WINDOW // rg
    mine = lax.div(me, 2)
    first = tok * groups

    barrier = pltpu.get_barrier_semaphore()

    @pl.loop(1, n_head)
    def _(step):
        pl.semaphore_signal(
            barrier, inc=1, device_id=(tok, lax.rem(me + step, n_head)), device_id_type=MESH
        )

    @pl.loop(1, n_tok)
    def _(step):
        pl.semaphore_signal(
            barrier, inc=1, device_id=(lax.rem(tok + step, n_tok), me), device_id_type=MESH
        )

    def rows_of(index, size):
        return pl.ds(pl.multiple_of(index * size, size), size)

    def cols_of(index):
        return pl.ds(pl.multiple_of(index * DH, DH), DH)

    def scatter(src, dst, base, send, recv, source, target):
        return pltpu.make_async_remote_copy(
            src_ref=src.at[:, cols_of(target)],
            dst_ref=dst.at[rows_of(base * n_head + source, rd)],
            send_sem=send.at[target],
            recv_sem=recv.at[source],
            device_id=(tok, target),
            device_id_type=MESH,
        )

    def k_copy(source, target):
        return scatter(k_hbm, kv.at[0], tok, k_send, k_recv, source, target)

    def v_copy(source, target):
        return scatter(v_hbm, kv.at[1], tok, v_send, v_recv, source, target)

    def q_copy(source, target):
        return scatter(q_hbm, qw, 0, q_send, q_recv, source, target)

    def o_copy(source, target):
        return pltpu.make_async_remote_copy(
            src_ref=obuf.at[rows_of(target, rd)],
            dst_ref=out_hbm.at[:, cols_of(source)],
            send_sem=o_send.at[target],
            recv_sem=o_recv.at[source],
            device_id=(tok, target),
            device_id_type=MESH,
        )

    own_copies = (
        pltpu.make_async_copy(
            k_hbm.at[:, cols_of(me)], kv.at[0, rows_of(tok * n_head + me, rd)], own_sem.at[0]
        ),
        pltpu.make_async_copy(
            v_hbm.at[:, cols_of(me)], kv.at[1, rows_of(tok * n_head + me, rd)], own_sem.at[1]
        ),
        pltpu.make_async_copy(q_hbm.at[:, cols_of(me)], qw.at[rows_of(me, rd)], own_sem.at[2]),
    )
    for copy in own_copies:
        copy.start()

    pl.semaphore_wait(barrier, n_head - 1 + n_tok - 1)

    @pl.loop(1, n_head)
    def _(step):
        target = lax.rem(me + step, n_head)
        k_copy(me, target).start()
        v_copy(me, target).start()

    @pl.loop(1, n_head)
    def _(step):
        q_copy(me, lax.rem(me + step, n_head)).start()

    def r_copy(source, target):
        return pltpu.make_async_remote_copy(
            src_ref=rate_ref,
            dst_ref=rates.at[source],
            send_sem=r_send.at[target],
            recv_sem=r_recv.at[source],
            device_id=(target, me),
            device_id_type=MESH,
        )

    @pl.loop(1, n_tok)
    def _(step):
        r_copy(tok, lax.rem(tok + step, n_tok)).start()

    acc[...] = jnp.zeros_like(acc)
    rates[tok] = rate_ref[...]

    for copy in own_copies:
        copy.wait()

    def f_copy(source, target, group):
        rows = rows_of(source * groups + group, rg)
        return pltpu.make_async_remote_copy(
            src_ref=kv.at[:, rows],
            dst_ref=kv.at[:, rows],
            send_sem=f_send.at[target, group],
            recv_sem=f_recv.at[source, group],
            device_id=(target, me),
            device_id_type=MESH,
        )

    @pl.loop(1, n_tok)
    def _(step):
        r_copy(lax.rem(tok + step, n_tok), tok).wait_recv()

    def group_at(step):
        return lax.rem(mine - step + groups, groups)

    def wait_group(group, copies):
        for core in range(2):
            source = group * 2 + core

            @pl.when(source != me)
            def _():
                for copy in copies:
                    copy(source, me).wait_recv()

    def contribute(source, group):
        rows = rows_of(source * groups + group, rg)
        keys = kv[0, rows, :]
        values = kv[1, rows, :].astype(jnp.float32)
        rate = -jnp.broadcast_to(rates[source, :, rows_of(group, rg)], (128, rg)).T
        target = jnp.concatenate(
            [values[:, :128] * rate, values[:, 128:] * rate], axis=1
        )
        target = target.astype(jnp.bfloat16)
        gate = dot_nt(keys, w_ref[0, :, 0:DH])
        up = dot_nt(keys, w_ref[0, :, DH : 2 * DH])
        back = dot_nt(target, w_ref[0, :, 2 * DH :])
        sig = sigmoid(gate)
        silu = gate * sig
        slope = sig * (1.0 + gate * (1.0 - sig))
        hidden = (silu * up).astype(jnp.bfloat16)
        gate_grad = (back * up * slope).astype(jnp.bfloat16)
        up_grad = (back * silu).astype(jnp.bfloat16)
        keys_t = turned(keys)
        acc[0] += dot_nn(keys_t, gate_grad)
        acc[1] += dot_nn(keys_t, up_grad)
        acc[2] += dot_nn(turned(target), hidden)

    @pl.loop(0, groups + 1)
    def _(step):
        @pl.loop(0, n_tok)
        def _(hop):
            source = lax.rem(tok + hop, n_tok)
            own = hop == 0
            group = group_at(jnp.where(own, step, step - 1))

            @pl.when(jnp.logical_and(own, step < groups))
            def _():
                wait_group(group, (k_copy, v_copy))

                @pl.loop(1, n_tok)
                def _(other):
                    f_copy(tok, lax.rem(tok + other, n_tok), group).start()

            @pl.when(jnp.logical_and(hop > 0, step > 0))
            def _():
                f_copy(source, tok, group).wait_recv()

            @pl.when(jnp.where(own, step < groups, step > 0))
            def _():
                contribute(source, group)

    row = lax.broadcasted_iota(jnp.int32, (rg, rg), 0)
    col = lax.broadcasted_iota(jnp.int32, (rg, rg), 1)

    def seen_chunk(group, chunk):
        return jnp.maximum(first + group + chunk - halo_groups, 0)

    def attend(group):
        wait_group(group, (q_copy,))
        queries = qw[rows_of(group, rg), :]
        scores = []
        for chunk in range(halo_groups + 1):
            value = dot_nt(queries, kv[0, rows_of(seen_chunk(group, chunk), rg), :])
            if chunk == 0:
                value = jnp.where(col > row, value, MASKED)
            if chunk == halo_groups:
                value = jnp.where(col <= row, value, MASKED)
            else:
                seen = first + group + chunk >= halo_groups
                value = value + jnp.where(seen, 0.0, MASKED)
            scores.append(value)
        highest = functools.reduce(jnp.maximum, scores)
        highest = jnp.max(highest, axis=1, keepdims=True)
        total = jnp.zeros((rg, rg), jnp.float32)
        result = jnp.zeros((rg, DH), jnp.float32)
        for chunk in range(halo_groups + 1):
            expo = jnp.exp2((scores[chunk] - highest) * (LOG2E * DH ** (-0.5)))
            total = total + expo
            result = result + dot_nn(
                expo.astype(jnp.bfloat16), kv[1, rows_of(seen_chunk(group, chunk), rg), :]
            )
        result = result / jnp.sum(total, axis=1, keepdims=True)
        return rms_norm(result)

    for block in range(3):
        total = acc[block]
        squares = jnp.sum(
            jnp.sum(total * total, axis=1, keepdims=True), axis=0, keepdims=True
        )
        zs[block] = (total * lax.rsqrt(squares + epsilon)).astype(jnp.bfloat16)

    @pl.loop(0, NS_STEPS)
    def _(step):
        blocks = [zs[block] for block in range(3)]
        grams = [dot_nt(z, z).astype(jnp.bfloat16) for z in blocks]
        polys = [
            (coef_cubic * a.astype(jnp.float32) + coef_quintic * dot_nn(a, a)).astype(
                jnp.bfloat16
            )
            for a in grams
        ]
        for block in range(3):
            zs[block] = (
                coef_linear * blocks[block].astype(jnp.float32)
                + dot_nn(polys[block], blocks[block])
            ).astype(jnp.bfloat16)

    for block in range(3):
        columns = slice(block * DH, (block + 1) * DH)
        wnew[:, columns] = (
            w_ref[0, :, columns].astype(jnp.float32) - zs[block].astype(jnp.float32).T
        ).astype(jnp.bfloat16)

    @pl.loop(0, groups)
    def _(step):
        group = group_at(step)
        attended = attend(group)
        queries = qw[rows_of(group, rg), :]
        gate = dot_nt(queries, wnew[:, 0:DH])
        up = dot_nt(queries, wnew[:, DH : 2 * DH])
        hidden = (gate * sigmoid(gate) * up).astype(jnp.bfloat16)
        applied = rms_norm(dot_nn(hidden, wnew[:, 2 * DH :]))
        obuf[rows_of(group, rg), :] = (attended + applied).astype(
            jnp.bfloat16
        )
        for core in range(2):
            target = group * 2 + core

            @pl.when(target != me)
            def _():
                o_copy(me, target).start()

    own_out = pltpu.make_async_copy(
        obuf.at[rows_of(me, rd)], out_hbm.at[:, cols_of(me)], own_sem.at[3]
    )
    own_out.start()
    owned = FH // n_tok
    neww_ref[0] = wnew[rows_of(tok, owned), :]

    @pl.loop(1, n_head)
    def _(step):
        target = lax.rem(me + step, n_head)
        k_copy(me, target).wait_send()
        v_copy(me, target).wait_send()
        q_copy(me, target).wait_send()
        o_copy(me, target).wait_send()

    @pl.loop(1, n_tok)
    def _(step):
        target = lax.rem(tok + step, n_tok)
        r_copy(tok, target).wait_send()

        @pl.loop(0, groups)
        def _(group):
            f_copy(tok, target, group).wait_send()

    @pl.loop(1, n_head)
    def _(step):
        o_copy(lax.rem(me + step, n_head), me).wait_recv()

    own_out.wait()


def per_device(query_states, key_states, value_states, token_rates, fast_weights):
    n_tok = lax.axis_size("tok")
    n_head = lax.axis_size("head")
    rd, width = query_states.shape
    rows = rd * n_head
    groups = n_head // 2
    dma = pltpu.SemaphoreType.DMA
    heads_sems = [dma((n_head,))] * 8
    return pl.pallas_call(
        functools.partial(layer_kernel, n_tok, n_head),
        out_shape=(
            jax.ShapeDtypeStruct((rd, width), jnp.bfloat16),
            jax.ShapeDtypeStruct((1, FH // n_tok, 3 * DH), jnp.bfloat16),
        ),
        in_specs=[pl.BlockSpec(memory_space=pl.ANY)] * 3
        + [pl.BlockSpec(memory_space=pltpu.VMEM)] * 2,
        out_specs=(
            pl.BlockSpec(memory_space=pl.ANY),
            pl.BlockSpec(memory_space=pltpu.VMEM),
        ),
        scratch_shapes=[
            pltpu.VMEM((2, n_tok * rows, DH), jnp.bfloat16),
            pltpu.VMEM((rows, DH), jnp.bfloat16),
            pltpu.VMEM((n_tok, 1, rows), jnp.float32),
            pltpu.VMEM((3, DH, FH), jnp.float32),
            pltpu.VMEM((3, DH, FH), jnp.bfloat16),
            pltpu.VMEM((FH, 3 * DH), jnp.bfloat16),
            pltpu.VMEM((rows, DH), jnp.bfloat16),
            dma((4,)),
            *heads_sems,
            dma((n_tok, groups)),
            dma((n_tok, groups)),
            dma((n_tok,)),
            dma((n_tok,)),
        ],
        compiler_params=pltpu.CompilerParams(
            collective_id=0, has_side_effects=True, vmem_limit_bytes=60 * 1024 * 1024
        ),
        name="layer",
    )(query_states, key_states, value_states, token_rates, fast_weights)


def solution(mesh):
    return jax.shard_map(
        per_device,
        mesh=mesh,
        in_specs=(
            P(("tok", "head"), None),
            P(("tok", "head"), None),
            P(("tok", "head"), None),
            P("head", "tok"),
            P("head", None, None),
        ),
        out_specs=(P(("tok", "head"), None), P("head", "tok", None)),
        check_vma=False,
    )
```

```python
import functools

import jax
import jax.numpy as jnp
from jax import lax
from jax.experimental import pallas as pl
from jax.experimental.pallas import tpu as pltpu
from jax.sharding import PartitionSpec as P

DH = 256
FH = 512
WINDOW = 1024
NS_STEPS = 5

coef_linear = 3.4445
coef_cubic = -4.775
coef_quintic = 2.0315
epsilon = 1e-06
LOG2E = 1.4426950408889634
MASKED = -1e30
MESH = pl.DeviceIdType.MESH


def dot_nt(left, right):
    return lax.dot_general(
        left, right, (((1,), (1,)), ((), ())), preferred_element_type=jnp.float32
    )


def dot_nn(left, right):
    return lax.dot_general(
        left, right, (((1,), (0,)), ((), ())), preferred_element_type=jnp.float32
    )


def rms_norm(values):
    return values * lax.rsqrt(jnp.mean(values * values, axis=-1, keepdims=True) + epsilon)


def sigmoid(values):
    return 1.0 / (1.0 + jnp.exp(-values))


def turned(values):
    return values.astype(jnp.float32).T.astype(jnp.bfloat16)


def layer_kernel(
    n_tok, n_head, q_hbm, k_hbm, v_hbm, rate_ref, w_ref,
    out_hbm, neww_ref,
    kv, qw, rates, acc, zs, wnew, obuf,
    own_sem, k_send, k_recv, v_send, v_recv, q_send, q_recv, o_send, o_recv,
    f_send, f_recv, r_send, r_recv,
):
    tok = lax.axis_index("tok")
    me = lax.axis_index("head")
    rd = q_hbm.shape[0]
    rg = 2 * rd
    groups = n_head // 2
    halo_groups = WINDOW // rg
    mine = lax.div(me, 2)
    first = tok * groups
    stride = 3 if groups % 3 else 1
    window = min(3, groups)

    barrier = pltpu.get_barrier_semaphore()

    @pl.loop(1, n_head)
    def _(step):
        pl.semaphore_signal(
            barrier, inc=1, device_id=(tok, lax.rem(me + step, n_head)), device_id_type=MESH
        )

    @pl.loop(1, n_tok)
    def _(step):
        pl.semaphore_signal(
            barrier, inc=1, device_id=(lax.rem(tok + step, n_tok), me), device_id_type=MESH
        )

    def rows_of(index, size):
        return pl.ds(pl.multiple_of(index * size, size), size)

    def cols_of(index):
        return pl.ds(pl.multiple_of(index * DH, DH), DH)

    def scatter(src, dst, base, send, recv, source, target):
        return pltpu.make_async_remote_copy(
            src_ref=src.at[:, cols_of(target)],
            dst_ref=dst.at[rows_of(base * n_head + source, rd)],
            send_sem=send.at[target],
            recv_sem=recv.at[source],
            device_id=(tok, target),
            device_id_type=MESH,
        )

    def k_copy(source, target):
        return scatter(k_hbm, kv.at[0], tok, k_send, k_recv, source, target)

    def v_copy(source, target):
        return scatter(v_hbm, kv.at[1], tok, v_send, v_recv, source, target)

    def q_copy(source, target):
        return scatter(q_hbm, qw, 0, q_send, q_recv, source, target)

    def o_copy(source, target):
        return pltpu.make_async_remote_copy(
            src_ref=obuf.at[rows_of(target, rd)],
            dst_ref=out_hbm.at[:, cols_of(source)],
            send_sem=o_send.at[target],
            recv_sem=o_recv.at[source],
            device_id=(tok, target),
            device_id_type=MESH,
        )

    own_copies = (
        pltpu.make_async_copy(
            k_hbm.at[:, cols_of(me)], kv.at[0, rows_of(tok * n_head + me, rd)], own_sem.at[0]
        ),
        pltpu.make_async_copy(
            v_hbm.at[:, cols_of(me)], kv.at[1, rows_of(tok * n_head + me, rd)], own_sem.at[1]
        ),
        pltpu.make_async_copy(q_hbm.at[:, cols_of(me)], qw.at[rows_of(me, rd)], own_sem.at[2]),
    )
    for copy in own_copies:
        copy.start()

    pl.semaphore_wait(barrier, n_head - 1 + n_tok - 1)

    def send(step, copies):
        for core in range(2):
            target = lax.rem(mine + stride * step, groups) * 2 + core

            @pl.when(target != me)
            def _():
                for copy in copies:
                    copy(me, target).start()

    @pl.loop(0, window)
    def _(step):
        send(step, (k_copy, v_copy))

    def r_copy(source, target):
        return pltpu.make_async_remote_copy(
            src_ref=rate_ref,
            dst_ref=rates.at[source],
            send_sem=r_send.at[target],
            recv_sem=r_recv.at[source],
            device_id=(target, me),
            device_id_type=MESH,
        )

    @pl.loop(1, n_tok)
    def _(step):
        r_copy(tok, lax.rem(tok + step, n_tok)).start()

    acc[...] = jnp.zeros_like(acc)
    rates[tok] = rate_ref[...]

    for copy in own_copies:
        copy.wait()

    def f_copy(source, target, group):
        rows = rows_of(source * groups + group, rg)
        return pltpu.make_async_remote_copy(
            src_ref=kv.at[:, rows],
            dst_ref=kv.at[:, rows],
            send_sem=f_send.at[target, group],
            recv_sem=f_recv.at[source, group],
            device_id=(target, me),
            device_id_type=MESH,
        )

    @pl.loop(1, n_tok)
    def _(step):
        r_copy(lax.rem(tok + step, n_tok), tok).wait_recv()

    def group_at(step):
        return lax.rem(mine + stride * (groups - step), groups)

    def wait_group(group, copies):
        for core in range(2):
            source = group * 2 + core

            @pl.when(source != me)
            def _():
                for copy in copies:
                    copy(source, me).wait_recv()

    def contribute(source, group):
        rows = rows_of(source * groups + group, rg)
        keys = kv[0, rows, :]
        values = kv[1, rows, :].astype(jnp.float32)
        rate = -jnp.broadcast_to(rates[source, :, rows_of(group, rg)], (128, rg)).T
        target = jnp.concatenate(
            [values[:, :128] * rate, values[:, 128:] * rate], axis=1
        )
        target = target.astype(jnp.bfloat16)
        gate = dot_nt(keys, w_ref[0, :, 0:DH])
        up = dot_nt(keys, w_ref[0, :, DH : 2 * DH])
        back = dot_nt(target, w_ref[0, :, 2 * DH :])
        sig = sigmoid(gate)
        silu = gate * sig
        slope = sig * (1.0 + gate * (1.0 - sig))
        hidden = (silu * up).astype(jnp.bfloat16)
        gate_grad = (back * up * slope).astype(jnp.bfloat16)
        up_grad = (back * silu).astype(jnp.bfloat16)
        keys_t = turned(keys)
        acc[0] += dot_nn(keys_t, gate_grad)
        acc[1] += dot_nn(keys_t, up_grad)
        acc[2] += dot_nn(turned(target), hidden)

    @pl.loop(0, groups + 1)
    def _(step):
        @pl.loop(0, n_tok)
        def _(hop):
            source = lax.rem(tok + hop, n_tok)
            own = hop == 0
            group = group_at(jnp.where(own, step, jnp.maximum(step - 1, 0)))

            @pl.when(jnp.logical_and(own, step < groups))
            def _():
                wait_group(group, (k_copy, v_copy))

                @pl.loop(1, n_tok)
                def _(other):
                    f_copy(tok, lax.rem(tok + other, n_tok), group).start()

                @pl.when(step + window < groups)
                def _():
                    send(step + window, (k_copy, v_copy))

                @pl.when(step == groups - window)
                def _():
                    @pl.loop(0, groups)
                    def _(later):
                        send(later, (q_copy,))

            @pl.when(jnp.logical_and(hop > 0, step > 0))
            def _():
                f_copy(source, tok, group).wait_recv()

            @pl.when(jnp.where(own, step < groups, step > 0))
            def _():
                contribute(source, group)

    row = lax.broadcasted_iota(jnp.int32, (rg, rg), 0)
    col = lax.broadcasted_iota(jnp.int32, (rg, rg), 1)

    def seen_chunk(group, chunk):
        return jnp.maximum(first + group + chunk - halo_groups, 0)

    def attend(group):
        wait_group(group, (q_copy,))
        queries = qw[rows_of(group, rg), :]
        scores = []
        for chunk in range(halo_groups + 1):
            value = dot_nt(queries, kv[0, rows_of(seen_chunk(group, chunk), rg), :])
            if chunk == 0:
                value = jnp.where(col > row, value, MASKED)
            if chunk == halo_groups:
                value = jnp.where(col <= row, value, MASKED)
            else:
                seen = first + group + chunk >= halo_groups
                value = value + jnp.where(seen, 0.0, MASKED)
            scores.append(value)
        highest = functools.reduce(jnp.maximum, scores)
        highest = jnp.max(highest, axis=1, keepdims=True)
        total = jnp.zeros((rg, rg), jnp.float32)
        result = jnp.zeros((rg, DH), jnp.float32)
        for chunk in range(halo_groups + 1):
            expo = jnp.exp2((scores[chunk] - highest) * (LOG2E * DH ** (-0.5)))
            total = total + expo
            result = result + dot_nn(
                expo.astype(jnp.bfloat16), kv[1, rows_of(seen_chunk(group, chunk), rg), :]
            )
        result = result / jnp.sum(total, axis=1, keepdims=True)
        return rms_norm(result)

    for block in range(3):
        total = acc[block]
        squares = jnp.sum(
            jnp.sum(total * total, axis=1, keepdims=True), axis=0, keepdims=True
        )
        zs[block] = (total * lax.rsqrt(squares + epsilon)).astype(jnp.bfloat16)

    @pl.loop(0, NS_STEPS)
    def _(step):
        blocks = [zs[block] for block in range(3)]
        grams = [dot_nt(z, z).astype(jnp.bfloat16) for z in blocks]
        polys = [
            (coef_cubic * a.astype(jnp.float32) + coef_quintic * dot_nn(a, a)).astype(
                jnp.bfloat16
            )
            for a in grams
        ]
        for block in range(3):
            zs[block] = (
                coef_linear * blocks[block].astype(jnp.float32)
                + dot_nn(polys[block], blocks[block])
            ).astype(jnp.bfloat16)

    for block in range(3):
        columns = slice(block * DH, (block + 1) * DH)
        wnew[:, columns] = (
            w_ref[0, :, columns].astype(jnp.float32) - zs[block].astype(jnp.float32).T
        ).astype(jnp.bfloat16)

    @pl.loop(0, groups)
    def _(step):
        group = group_at(step)
        attended = attend(group)
        queries = qw[rows_of(group, rg), :]
        gate = dot_nt(queries, wnew[:, 0:DH])
        up = dot_nt(queries, wnew[:, DH : 2 * DH])
        hidden = (gate * sigmoid(gate) * up).astype(jnp.bfloat16)
        applied = rms_norm(dot_nn(hidden, wnew[:, 2 * DH :]))
        obuf[rows_of(group, rg), :] = (attended + applied).astype(
            jnp.bfloat16
        )
        for core in range(2):
            target = group * 2 + core

            @pl.when(target != me)
            def _():
                o_copy(me, target).start()

    own_out = pltpu.make_async_copy(
        obuf.at[rows_of(me, rd)], out_hbm.at[:, cols_of(me)], own_sem.at[3]
    )
    own_out.start()
    owned = FH // n_tok
    neww_ref[0] = wnew[rows_of(tok, owned), :]

    @pl.loop(1, n_head)
    def _(step):
        target = lax.rem(me + step, n_head)
        k_copy(me, target).wait_send()
        v_copy(me, target).wait_send()
        q_copy(me, target).wait_send()
        o_copy(me, target).wait_send()

    @pl.loop(1, n_tok)
    def _(step):
        target = lax.rem(tok + step, n_tok)
        r_copy(tok, target).wait_send()

        @pl.loop(0, groups)
        def _(group):
            f_copy(tok, target, group).wait_send()

    @pl.loop(1, n_head)
    def _(step):
        o_copy(lax.rem(me + step, n_head), me).wait_recv()

    own_out.wait()


def per_device(query_states, key_states, value_states, token_rates, fast_weights):
    n_tok = lax.axis_size("tok")
    n_head = lax.axis_size("head")
    rd, width = query_states.shape
    rows = rd * n_head
    groups = n_head // 2
    dma = pltpu.SemaphoreType.DMA
    heads_sems = [dma((n_head,))] * 8
    return pl.pallas_call(
        functools.partial(layer_kernel, n_tok, n_head),
        out_shape=(
            jax.ShapeDtypeStruct((rd, width), jnp.bfloat16),
            jax.ShapeDtypeStruct((1, FH // n_tok, 3 * DH), jnp.bfloat16),
        ),
        in_specs=[pl.BlockSpec(memory_space=pl.ANY)] * 3
        + [pl.BlockSpec(memory_space=pltpu.VMEM)] * 2,
        out_specs=(
            pl.BlockSpec(memory_space=pl.ANY),
            pl.BlockSpec(memory_space=pltpu.VMEM),
        ),
        scratch_shapes=[
            pltpu.VMEM((2, n_tok * rows, DH), jnp.bfloat16),
            pltpu.VMEM((rows, DH), jnp.bfloat16),
            pltpu.VMEM((n_tok, 1, rows), jnp.float32),
            pltpu.VMEM((3, DH, FH), jnp.float32),
            pltpu.VMEM((3, DH, FH), jnp.bfloat16),
            pltpu.VMEM((FH, 3 * DH), jnp.bfloat16),
            pltpu.VMEM((rows, DH), jnp.bfloat16),
            dma((4,)),
            *heads_sems,
            dma((n_tok, groups)),
            dma((n_tok, groups)),
            dma((n_tok,)),
            dma((n_tok,)),
        ],
        compiler_params=pltpu.CompilerParams(
            collective_id=0, has_side_effects=True, vmem_limit_bytes=60 * 1024 * 1024
        ),
        name="layer",
    )(query_states, key_states, value_states, token_rates, fast_weights)


def solution(mesh):
    return jax.shard_map(
        per_device,
        mesh=mesh,
        in_specs=(
            P(("tok", "head"), None),
            P(("tok", "head"), None),
            P(("tok", "head"), None),
            P("head", "tok"),
            P("head", None, None),
        ),
        out_specs=(P(("tok", "head"), None), P("head", "tok", None)),
        check_vma=False,
    )
```
